32 devices in a mesh: seq: 4 (over z), tp: 4 (over y, x), fsdp: 2 (over core).
Axes of the slice: x: 2, y: 2, z: 4, core: 2. Of those that a mesh axis runs over, the one named last changes fastest.
Arguments:
- decoder_in: bfloat16 [32, 128, 1024], P(('seq', 'fsdp')), may hold values from -6 to 6
- memory: bfloat16 [32, 2048, 1024], P(('seq', 'fsdp')), may hold values from -6 to 6
- buckets: int32 [128, 128], replicated, may hold values from 0 to 31
- norm_gains: bfloat16 [3, 1024], P(None, ('seq', 'fsdp')), may hold values from 0.5 to 1.5
- rel_bias: bfloat16 [32, 16], P(('seq', 'fsdp'), 'tp'), may hold values from -4 to 4
- self_q: bfloat16 [1024, 1024], P(('seq', 'fsdp'), 'tp'), may hold values from -0.1875 to 0.1875
- self_kv: bfloat16 [1024, 2, 512], P(('seq', 'fsdp'), None, 'tp'), may hold values from -0.1875 to 0.1875
- self_out: bfloat16 [1024, 1024], P('tp', ('seq', 'fsdp')), may hold values from -0.75 to 0.75
- cross_q: bfloat16 [1024, 1024], P(('seq', 'fsdp'), 'tp'), may hold values from -0.1875 to 0.1875
- cross_kv: bfloat16 [1024, 2, 512], P(('seq', 'fsdp'), None, 'tp'), may hold values from -0.1875 to 0.1875
- cross_out: bfloat16 [1024, 1024], P('tp', ('seq', 'fsdp')), may hold values from -3 to 3
- gate_up: bfloat16 [1024, 2, 2816], P(('seq', 'fsdp'), None, 'tp'), may hold values from -0.1875 to 0.1875
- down: bfloat16 [2816, 1024], P('tp', ('seq', 'fsdp')), may hold values from -0.109375 to 0.109375
- cotangent: bfloat16 [32, 128, 1024], P(('seq', 'fsdp')), may hold values from -6 to 6
Outputs:
- decoder_out: bfloat16 [32, 128, 1024], P(('seq', 'fsdp'))
- decoder_grad: float32 [32, 128, 1024], P(('seq', 'fsdp'))
- memory_grad: bfloat16 [32, 2048, 1024], P(('seq', 'fsdp'), None, 'tp')
- gains_grad: float32 [3, 1024], P(None, ('seq', 'fsdp'))
- bias_grad: float32 [32, 16], P(('seq', 'fsdp'), 'tp')
- self_q_grad: float32 [1024, 1024], P(('seq', 'fsdp'), 'tp')
- self_kv_grad: float32 [1024, 2, 512], P(('seq', 'fsdp'), None, 'tp')
- self_out_grad: float32 [1024, 1024], P('tp', ('seq', 'fsdp'))
- cross_q_grad: float32 [1024, 1024], P(('seq', 'fsdp'), 'tp')
- cross_kv_grad: float32 [1024, 2, 512], P(('seq', 'fsdp'), None, 'tp')
- cross_out_grad: float32 [1024, 1024], P('tp', ('seq', 'fsdp'))
- gate_up_grad: float32 [1024, 2, 2816], P(('seq', 'fsdp'), None, 'tp')
- down_grad: float32 [2816, 1024], P('tp', ('seq', 'fsdp'))
The draws below stay inside these ranges and needn't reach their ends.
Inputs may be any that keep to these rules, and one draw needn't show every extreme that they name: `buckets`: the bucket of query position i and key position j, the same for every sequence and head.
All inputs are finite; a program needn't handle non-finite values.
Results may differ from the reference program's by a relative error of at most 0.04.
Values may be sent and summed in bfloat16 or wider, within the bound.
No kernel may reach another device: no remote copies, remote signals or barrier semaphores. Data moves between devices by JAX's collectives and lax.ppermute only.
A program may use at most 192 MiB of HBM per device.

```python
import jax
import jax.numpy as jnp
from jax import lax

D = 1024
H = 16
DH = 64
G = 8
FF = 2816
NB = 32
LEN = 128
MEM = 2048
SEQS = 32


def set_ends(array, own_key, least, top_value):
    dims = array.shape
    index_at = [jax.random.randint(jax.random.fold_in(own_key, axis), (), 0, dims[axis]) for axis in range(len(dims))]
    array = array.at[tuple(index_at)].set(least)
    longest = dims.index(max(dims))
    index_at[longest] = (index_at[longest] + 1) % dims[longest]
    return array.at[tuple(index_at)].set(top_value)


def spiked(result, rng, source, target, parts, factor):
    owner, partner = [(jnp.arange(result.shape[dim]) // (result.shape[dim] // parts)).reshape([-1 if axis == dim else 1 for axis in range(result.ndim)]) for dim in (source, target)]
    chosen = jax.random.permutation(rng, parts)[partner]
    strong = (owner == chosen) | (owner == (partner + parts // 2) % parts)
    return jnp.where(strong, factor * result, result)


def level_of(key, dims, cuts, smallest, high):
    level = 1.0
    for axis_at, blocks in cuts:
        draws = jax.random.uniform(jax.random.fold_in(jax.random.fold_in(key, 6), axis_at), (blocks,), jnp.float32, smallest / len(cuts), high / len(cuts))
        level = level * jnp.repeat(jnp.exp(draws), dims[axis_at] // blocks).reshape((-1,) + (1,) * (len(dims) - 1 - axis_at))
    return level


def normal_values(stream_key, shape, width, bound, pieces=(), kind=jnp.bfloat16):
    values = width * jax.random.normal(stream_key, shape, jnp.float32)
    if pieces:
        values = values * level_of(stream_key, shape, pieces, -0.22, 0.18)
    return jnp.clip(values, -bound, bound).astype(kind)


def noise_with(stream_key, extent, deviation, bound, shards, heavy, kind=jnp.bfloat16):
    result = deviation * jax.random.normal(stream_key, extent, jnp.float32)
    if shards:
        result = result * level_of(stream_key, extent, shards, -0.22, 0.18)
    return jnp.clip(spiked(result, jax.random.fold_in(stream_key, 3), *heavy), -bound, bound).astype(kind)


def setup_inputs(seed: int = 0) -> dict:
    seeds = jax.random.split(jax.random.key(seed), 15)
    return {
        "decoder_in": normal_values(seeds[0], (SEQS, LEN, D), 1.0, 6.0, ((0, 8),)),
        "memory": normal_values(seeds[1], (SEQS, MEM, D), 1.0, 6.0, ((0, 8),)),
        "buckets": set_ends(jax.random.randint(seeds[2], (LEN, LEN), 0, NB), jax.random.fold_in(seeds[2], 1), 0, NB - 1).astype(jnp.int32),
        "norm_gains": jnp.clip(1.0 + 0.1 * jax.random.normal(seeds[3], (3, D), jnp.float32), 0.5, 1.5).astype(jnp.bfloat16),
        "rel_bias": normal_values(seeds[4], (NB, H), 1.0, 4.0, ((0, 8), (1, 4))),
        "self_q": normal_values(seeds[5], (D, H * DH), D ** -0.5, 0.1875, ((0, 8), (1, 4))),
        "self_kv": normal_values(seeds[6], (D, 2, G * DH), D ** -0.5, 0.1875, ((0, 8), (2, 4))),
        "self_out": normal_values(seeds[7], (H * DH, D), (H * DH * 8 // LEN) ** -0.5, 0.75, ((0, 4), (1, 8))),
        "cross_q": normal_values(seeds[8], (D, H * DH), D ** -0.5, 0.1875, ((0, 8), (1, 4))),
        "cross_kv": normal_values(seeds[9], (D, 2, G * DH), D ** -0.5, 0.1875, ((0, 8), (2, 4))),
        "cross_out": normal_values(seeds[10], (H * DH, D), (H * DH * 8 // MEM) ** -0.5, 3.0, ((0, 4), (1, 8))),
        "gate_up": normal_values(seeds[11], (D, 2, FF), D ** -0.5, 0.1875, ((0, 8), (2, 4))),
        "down": normal_values(seeds[12], (FF, D), FF ** -0.5, 0.109375, ((0, 4), (1, 8))),
        "cotangent": noise_with(seeds[13], (SEQS, LEN, D), 1.0, 6.0, ((0, 8),), (0, 2, 8, 2.0)),
    }


@jax.custom_vjp
def low(v):
    return lax.optimization_barrier(v.astype(jnp.bfloat16)).astype(jnp.float32)

@jax.custom_vjp
def low_back(v):
    return v

def low_keep(v):
    return (low(v), None)

def low_pass(kept, grad):
    return (grad,)

def back_keep(v):
    return (v, None)

def back_low(kept, grad):
    return (low(grad),)
low.defvjp(low_keep, low_pass)
low_back.defvjp(back_keep, back_low)
HIGHEST = lax.Precision.HIGHEST
EPSILON = 1e-06
MASKED = -1e+30

def both_ways(values):
    return low_back(low(values))

def rms_norm(values, gain):
    return values * lax.rsqrt(lax.optimization_barrier(jnp.mean(values * values, axis=-1, keepdims=True)) + EPSILON) * gain

def attend(query, keys, values, bias, causal):
    rows = query.shape[0]
    span = keys.shape[0]
    query_heads = query.reshape(rows, H, DH)
    key_heads = jnp.repeat(keys.reshape(span, G, DH), H // G, axis=1)
    value_heads = jnp.repeat(values.reshape(span, G, DH), H // G, axis=1)
    scores = jnp.einsum('ihd,jhd->hij', query_heads, key_heads, precision=HIGHEST) * DH ** (-0.5)
    if bias is not None:
        scores = scores + bias
    scores = low_back(scores)
    if causal is not None:
        scores = jnp.where(causal, scores, MASKED)
    row_max = lax.optimization_barrier(jnp.max(scores, axis=-1, keepdims=True))
    exponent = jnp.exp(scores - row_max)
    probs = exponent / lax.optimization_barrier(jnp.sum(exponent, axis=-1, keepdims=True))
    mixed = jnp.einsum('hij,jhd->ihd', low(probs), value_heads, precision=HIGHEST)
    return mixed.reshape(rows, H * DH)

def layer(tokens, memory, weights, onehot, causal):
    gains, table, self_q, self_kv, self_out, cross_q, cross_kv, cross_out, gate_up, down = weights
    normed = low(rms_norm(tokens, gains[0]))
    query = both_ways(jnp.dot(normed, self_q, precision=HIGHEST))
    keys = both_ways(jnp.dot(normed, self_kv[:, 0], precision=HIGHEST))
    values = both_ways(jnp.dot(normed, self_kv[:, 1], precision=HIGHEST))
    bias = jnp.einsum('ijn,nh->hij', onehot, table, precision=HIGHEST)
    mixed = both_ways(attend(query, keys, values, bias, causal))
    after_self = tokens + low_back(jnp.dot(mixed, self_out, precision=HIGHEST))
    normed = low(rms_norm(after_self, gains[1]))
    query = both_ways(jnp.dot(normed, cross_q, precision=HIGHEST))
    keys = both_ways(jnp.dot(memory, cross_kv[:, 0], precision=HIGHEST))
    values = both_ways(jnp.dot(memory, cross_kv[:, 1], precision=HIGHEST))
    mixed = both_ways(attend(query, keys, values, None, None))
    after_cross = after_self + low_back(jnp.dot(mixed, cross_out, precision=HIGHEST))
    normed = low(rms_norm(after_cross, gains[2]))
    gate = low_back(jnp.dot(normed, gate_up[:, 0], precision=HIGHEST))
    up = low_back(jnp.dot(normed, gate_up[:, 1], precision=HIGHEST))
    hidden = low(jax.nn.gelu(gate, approximate=True) * up)
    return after_cross + low_back(jnp.dot(hidden, down, precision=HIGHEST))

def reference(decoder_in, memory, buckets, norm_gains, rel_bias, self_q, self_kv, self_out, cross_q, cross_kv, cross_out, gate_up, down, cotangent):
    weights = tuple((weight.astype(jnp.float32) for weight in (norm_gains, rel_bias, self_q, self_kv, self_out, cross_q, cross_kv, cross_out, gate_up, down)))
    positions = jnp.arange(LEN, dtype=jnp.int32)
    causal = positions[:, None] >= positions[None, :]
    onehot = (buckets[:, :, None] == jnp.arange(NB, dtype=jnp.int32)[None, None, :]).astype(jnp.float32)

    def one_sequence(totals, inputs):
        sequence_tokens, sequence_memory, sequence_grad = inputs

        def forward(tokens, memory_rows, weight_set):
            return layer(tokens, memory_rows, weight_set, onehot, causal)
        output, pull = jax.vjp(forward, sequence_tokens.astype(jnp.float32), sequence_memory.astype(jnp.float32), weights)
        grad_tokens, grad_memory, grad_weights = pull(sequence_grad.astype(jnp.float32))
        totals = jax.tree.map(jnp.add, totals, grad_weights)
        return (totals, (output.astype(jnp.bfloat16), grad_tokens, grad_memory.astype(jnp.bfloat16)))
    start = jax.tree.map(jnp.zeros_like, weights)
    totals, (outputs, token_grads, memory_grads) = lax.scan(one_sequence, start, (decoder_in, memory, cotangent))
    return (outputs, token_grads, memory_grads, totals[0], totals[1], totals[2], totals[3], totals[4], totals[5], totals[6], totals[7], totals[8], totals[9])
```

```python
import jax
import jax.numpy as jnp
from jax import lax
from jax.sharding import PartitionSpec as P

DH = 64
NB = 32
EPSILON = 1e-06
MASKED = -1e30
F32 = jnp.float32
BF16 = jnp.bfloat16


def rms_norm(values, gain):
    return values * lax.rsqrt(jnp.mean(values * values, axis=-1, keepdims=True) + EPSILON) * gain


def gelu_product(gate, up):
    return jax.nn.gelu(gate, approximate=True) * up


def mm(a, b, dims):
    return lax.dot_general(a, b, (dims, ((), ())), preferred_element_type=F32)


def split_heads(query, keys, values):
    batch, rows, width = query.shape
    span = keys.shape[1]
    groups = keys.shape[2] // DH
    ratio = width // DH // groups
    return (
        query.reshape(batch, rows, groups, ratio, DH),
        keys.reshape(batch, span, groups, DH),
        values.reshape(batch, span, groups, DH),
    )


def scores_of(query_heads, key_heads, bias, causal):
    scores = jnp.einsum(
        "bigrd,bjgd->bgrij", query_heads, key_heads, preferred_element_type=F32
    ) * DH ** (-0.5)
    if bias is not None:
        scores = scores + bias
    if causal is not None:
        scores = jnp.where(causal, scores, MASKED)
    return scores


def attend_forward(query, keys, values, bias, causal):
    query_heads, key_heads, value_heads = split_heads(query, keys, values)
    scores = scores_of(query_heads, key_heads, bias, causal)
    row_max = jnp.max(scores, axis=-1, keepdims=True)
    exponent = jnp.exp(scores - row_max)
    total = jnp.sum(exponent, axis=-1, keepdims=True)
    probs = (exponent / total).astype(BF16)
    mixed = jnp.einsum("bgrij,bjgd->bigrd", probs, value_heads, preferred_element_type=F32)
    return (mixed.reshape(query.shape).astype(BF16), row_max + jnp.log(total))


def attend_backward(query, keys, values, bias, causal, log_total, grad_mixed):
    query_heads, key_heads, value_heads = split_heads(query, keys, values)
    probs = jnp.exp(scores_of(query_heads, key_heads, bias, causal) - log_total)
    grad_heads = grad_mixed.reshape(query_heads.shape)
    grad_probs = jnp.einsum("bigrd,bjgd->bgrij", grad_heads, value_heads, preferred_element_type=F32)
    inner = jnp.sum(probs * grad_probs, axis=-1, keepdims=True)
    grad_scores = (probs * (grad_probs - inner)).astype(BF16)
    scale = DH ** (-0.5)
    grad_query = (
        jnp.einsum("bgrij,bjgd->bigrd", grad_scores, key_heads, preferred_element_type=F32) * scale
    ).astype(BF16)
    grad_keys = (
        jnp.einsum("bgrij,bigrd->bjgd", grad_scores, query_heads, preferred_element_type=F32)
        * scale
    ).astype(BF16)
    grad_values = jnp.einsum(
        "bgrij,bigrd->bjgd", probs.astype(BF16), grad_heads, preferred_element_type=F32
    ).astype(BF16)
    return (
        grad_query.reshape(query.shape),
        grad_keys.reshape(keys.shape),
        grad_values.reshape(values.shape),
        grad_scores,
    )


def per_device(
    decoder_in,
    memory,
    buckets,
    norm_gains,
    rel_bias,
    self_q,
    self_kv,
    self_out,
    cross_q,
    cross_kv,
    cross_out,
    gate_up,
    down,
    cotangent,
    tp_size,
    seq_size,
):
    batch, rows, width = decoder_in.shape
    split = tp_size // batch
    if batch * split != tp_size or rows % split:
        raise ValueError("unsupported mesh")
    chunk = rows // split
    t = lax.axis_index("tp")
    f = lax.axis_index("fsdp")
    s = lax.axis_index("seq")
    zf = ("seq", "fsdp")

    def swap_tp(x, j):
        return lax.ppermute(x, "tp", [(i, i ^ j) for i in range(tp_size)])

    def swap_core(x):
        return lax.ppermute(x, "fsdp", [(0, 1), (1, 0)])

    def exchange(pieces):
        return [pieces[0]] + [swap_tp(pieces[j], j) for j in range(1, tp_size)]

    def spread(x):
        return [x] + [swap_tp(x, j) for j in range(1, tp_size)]

    def relative(x, member, count):
        return jnp.stack([lax.dynamic_index_in_dim(x, member ^ j, 0, False) for j in range(count)])

    def piece(x, j):
        part = x[j // split]
        if split == 1:
            return part
        return lax.dynamic_slice_in_dim(part, ((t % split) ^ (j % split)) * chunk, chunk, 0)

    def pieces_of(x):
        return [piece(x, j) for j in range(tp_size)]

    def whole_rows(pieces):
        if split == 1:
            return jnp.stack(pieces)
        out = []
        for b in range(batch):
            own = jnp.stack(pieces[b * split : (b + 1) * split])
            own = relative(own, t % split, split)
            out.append(own.reshape((rows,) + own.shape[2:]))
        return jnp.stack(out)

    def placed(pieces):
        out = jnp.zeros((tp_size,) + pieces[0].shape, pieces[0].dtype)
        for j in range(tp_size):
            out = lax.dynamic_update_index_in_dim(out, pieces[j], t ^ j, 0)
        return out

    def rejoin(own, other):
        first = jnp.where(f == 0, own, other)
        second = jnp.where(f == 0, other, own)
        full = jnp.stack([first, second], axis=1)
        return full.reshape(-1, full.shape[-1])

    shard = self_q.shape[0]
    extra = jnp.zeros((4, shard), BF16)
    extra = extra.at[:3].set(norm_gains)
    tb_rows, heads = rel_bias.shape
    extra = extra.at[3, : tb_rows * heads].set(rel_bias.reshape(-1))
    extra = lax.all_gather(extra, zf, axis=0, tiled=False)
    gains = jnp.transpose(extra[:, :3], (1, 0, 2)).reshape(3, -1).astype(F32)
    table = extra[:, 3, : tb_rows * heads].reshape(NB, heads)

    pack_full = jnp.stack(
        [
            jnp.concatenate([self_out.T, cross_kv.reshape(shard, -1)], axis=1),
            jnp.concatenate([cross_q, cross_out.T], axis=1),
        ]
    )
    got_full = lax.all_gather(pack_full, "seq", axis=0, tiled=False)
    pack_self = jnp.concatenate([self_q, self_kv.reshape(shard, -1)], axis=1)
    w_self = lax.all_gather(pack_self, zf, axis=0, tiled=True)
    pack_ffn = jnp.concatenate([gate_up.reshape(shard, -1), down.T], axis=1)
    w_ffn = lax.all_gather(pack_ffn, zf, axis=0, tiled=True)

    cols = self_q.shape[1]

    def full_pair(index):
        part = got_full[:, index]
        mine = spread(part)
        theirs = [swap_core(p) for p in mine]
        joined = [rejoin(a, b) for a, b in zip(mine, theirs)]
        first = jnp.concatenate([w[:, :cols] for w in joined], axis=1)
        second = jnp.concatenate([w[:, cols:] for w in joined], axis=1)
        return first, second

    w_so, w_ckv = full_pair(0)
    w_cq, w_co = full_pair(1)

    positions = jnp.arange(rows, dtype=jnp.int32)
    causal = positions[:, None] >= positions[None, :]
    onehot = (buckets[:, :, None] == jnp.arange(NB, dtype=jnp.int32)[None, None, :]).astype(BF16)
    kv_half = self_kv.shape[2]
    groups = kv_half // DH
    bias = jnp.einsum("ijn,nh->hij", onehot, table, preferred_element_type=F32).reshape(
        groups, heads // groups, rows, rows
    )

    tokens = relative(decoder_in, t // split, batch)
    start = tokens.astype(F32)
    normed_self = rms_norm(start, gains[0]).astype(BF16)
    proj = mm(normed_self, w_self, (((2,), (0,)))).astype(BF16)
    query_self = proj[..., :cols]
    keys_self = proj[..., cols : cols + kv_half]
    values_self = proj[..., cols + kv_half :]
    mixed_self, log_self = attend_forward(query_self, keys_self, values_self, bias, causal)
    o1 = jnp.concatenate(exchange(pieces_of(mixed_self)), axis=-1)

    x0 = piece(start, 0)
    x1 = x0 + mm(o1, w_so, ((1,), (1,)))
    n2 = rms_norm(x1, gains[1]).astype(BF16)
    q2 = mm(n2, w_cq, ((1,), (0,))).astype(BF16)
    own_memory = lax.dynamic_index_in_dim(memory, t // split, 0, False)
    kv2 = mm(own_memory, w_ckv, ((1,), (0,))).astype(BF16)
    span = kv2.shape[0]
    kv2 = kv2.reshape(span, tp_size, 2, kv_half)
    k2 = kv2[:, :, 0].reshape(1, span, -1)
    v2 = kv2[:, :, 1].reshape(1, span, -1)
    o2, log_cross = attend_forward(q2[None], k2, v2, None, None)
    x2 = x1 + mm(o2[0], w_co, ((1,), (1,)))
    n3 = rms_norm(x2, gains[2]).astype(BF16)

    n3_all = jnp.stack(spread(n3)).reshape(-1, width)
    ff2 = gate_up.shape[2] * 2
    hid = gate_up.shape[2]
    w_gu = w_ffn[:, :ff2]
    w_dn = w_ffn[:, ff2:]
    joined = mm(n3_all, w_gu, ((1,), (0,)))
    gate = joined[:, :hid]
    up = joined[:, hid:]
    hidden = gelu_product(gate, up).astype(BF16)
    out_part = mm(hidden, w_dn, ((1,), (1,))).astype(BF16).reshape(tp_size, chunk, width)

    cot = relative(cotangent.reshape(tp_size, chunk, width), t, tp_size)
    y3 = cot.reshape(-1, width)
    grad_hidden = mm(y3, w_dn, ((1,), (0,)))
    _, pull = jax.vjp(gelu_product, gate, up)
    grad_gate, grad_up = pull(grad_hidden)
    grad_joined = jnp.concatenate([grad_gate, grad_up], axis=-1).astype(BF16)
    dn3_part = mm(grad_joined, w_gu, ((1,), (1,))).astype(BF16).reshape(tp_size, chunk, width)

    def total(pieces):
        acc = pieces[0].astype(F32)
        for p in pieces[1:]:
            acc = acc + p.astype(F32)
        return acc

    dn3 = total(exchange([dn3_part[j] for j in range(tp_size)]))
    out = x2 + total(exchange([out_part[j] for j in range(tp_size)]))
    decoder_out = placed(spread(out.astype(BF16))).reshape(decoder_in.shape)

    gu_grad = mm(n3_all, grad_joined, ((0,), (0,))).astype(BF16)
    dn_grad = mm(y3, hidden, ((0,), (0,))).astype(BF16)
    ffn_grad = lax.psum_scatter(
        jnp.concatenate([gu_grad, dn_grad], axis=1), zf, scatter_dimension=0, tiled=True
    )

    e3 = cot[0].astype(F32)
    _, pull = jax.vjp(rms_norm, x2, gains[2])
    dv, dg2 = pull(dn3)
    e2 = e3 + dv
    y2 = e2.astype(BF16)
    do2 = mm(y2, w_co, ((1,), (0,))).astype(BF16)
    dq2, dk2, dv2, _ = attend_backward(q2[None], k2, v2, None, None, log_cross, do2[None])
    dq2 = dq2[0]
    dkv2 = jnp.stack(
        [dk2[0].reshape(span, tp_size, kv_half), dv2[0].reshape(span, tp_size, kv_half)], axis=2
    ).reshape(span, -1)
    dn2 = mm(dq2, w_cq, ((1,), (1,)))
    _, pull = jax.vjp(rms_norm, x1, gains[1])
    dv, dg1 = pull(dn2)
    e1 = e2 + dv
    y1 = e1.astype(BF16)
    do1_full = mm(y1, w_so, ((1,), (0,))).astype(BF16)
    do1 = whole_rows(exchange([do1_full[:, j * cols : (j + 1) * cols] for j in range(tp_size)]))

    quarter = width // tp_size
    w_rows = w_ckv.reshape(tp_size, quarter, -1)
    mem_pieces = []
    for j in range(tp_size):
        w_j = lax.dynamic_index_in_dim(w_rows, t ^ j, 0, False)
        mem_pieces.append(mm(dkv2, w_j, ((1,), (1,))).astype(BF16))
    mem_got = exchange(mem_pieces)
    memory_grad = jnp.zeros((batch,) + mem_got[0].shape, BF16)
    for b in range(batch):
        own = mem_got[b * split]
        if split > 1:
            own = total(mem_got[b * split : (b + 1) * split]).astype(BF16)
        memory_grad = lax.dynamic_update_index_in_dim(memory_grad, own, (t // split) ^ b, 0)

    def core_sum(grad):
        g = grad.reshape(seq_size, 2, shard, -1)
        mine = lax.dynamic_index_in_dim(g, f, 1, False)
        theirs = lax.dynamic_index_in_dim(g, 1 - f, 1, False)
        return (mine.astype(F32) + swap_core(theirs).astype(F32)).astype(BF16)

    def tp_sum(parts):
        pieces = [
            jnp.concatenate([p[..., j * cols : (j + 1) * cols] for p in parts], axis=-1)
            for j in range(tp_size)
        ]
        return total(exchange(pieces)).astype(BF16)

    g_co = core_sum(mm(y2, o2[0], ((0,), (0,))).astype(BF16))
    g_cq = core_sum(mm(n2, dq2, ((0,), (0,))).astype(BF16))
    g_ckv = core_sum(mm(own_memory, dkv2, ((0,), (0,))).astype(BF16))
    g_so = core_sum(mm(y1, o1, ((0,), (0,))).astype(BF16))
    full_grad = tp_sum([g_co, g_cq, g_ckv, g_so])
    full_grad = lax.psum_scatter(full_grad, "seq", scatter_dimension=0, tiled=False)

    dq1, dk1, dv1, ds1 = attend_backward(
        query_self, keys_self, values_self, bias, causal, log_self, do1
    )
    table_grad = jnp.einsum(
        "ijn,bhij->nh", onehot, ds1.reshape(batch, -1, rows, rows), preferred_element_type=F32
    )
    dproj = jnp.concatenate([dq1, dk1, dv1], axis=-1)
    dn1_part = mm(dproj, w_self, ((2,), (1,))).astype(BF16)
    self_grad = lax.psum_scatter(
        mm(normed_self.reshape(-1, width), dproj.reshape(-1, dproj.shape[-1]), ((0,), (0,))).astype(
            BF16
        ),
        zf,
        scatter_dimension=0,
        tiled=True,
    )
    dn1 = total(exchange(pieces_of(dn1_part)))
    _, pull = jax.vjp(rms_norm, x0, gains[0])
    dv, dg0 = pull(dn1)
    decoder_grad = placed(spread((e1 + dv).astype(BF16))).reshape(decoder_in.shape).astype(F32)

    small = jnp.stack([dg0, dg1, dg2, jnp.pad(table_grad.reshape(-1), (0, width - NB * heads))])
    small = lax.all_gather(small, ("seq", "fsdp", "tp"), axis=0, tiled=False)
    place = s * 2 + f
    gains_grad = lax.dynamic_slice_in_dim(jnp.sum(small[:, :3], axis=0), place * shard, shard, 1)
    tables = small[:, 3, : NB * heads].reshape(-1, tp_size, NB * heads)
    tables = jnp.sum(lax.dynamic_index_in_dim(tables, t, 1, False), axis=0).reshape(NB, heads)
    bias_grad = lax.dynamic_slice_in_dim(tables, place * tb_rows, tb_rows, 0)

    full_grad = full_grad.astype(F32)
    self_grad = self_grad.astype(F32)
    ffn_grad = ffn_grad.astype(F32)
    return (
        decoder_out,
        decoder_grad,
        memory_grad,
        gains_grad,
        bias_grad,
        self_grad[:, :cols],
        self_grad[:, cols:].reshape(self_kv.shape),
        full_grad[:, 3 * cols :].T,
        full_grad[:, cols : 2 * cols],
        full_grad[:, 2 * cols : 3 * cols].reshape(cross_kv.shape),
        full_grad[:, :cols].T,
        ffn_grad[:, :ff2].reshape(gate_up.shape),
        ffn_grad[:, ff2:].T,
    )


def solution(mesh):
    tp_size = mesh.shape["tp"]
    seq_size = mesh.shape["seq"]

    def body(*args):
        return per_device(*args, tp_size=tp_size, seq_size=seq_size)

    both = ("seq", "fsdp")
    token = P(both, None, None)
    weight = P(both, "tp")
    paired = P(both, None, "tp")
    turned = P("tp", both)
    return jax.shard_map(
        body,
        mesh=mesh,
        in_specs=(
            token,
            token,
            P(),
            P(None, both),
            weight,
            weight,
            paired,
            turned,
            weight,
            paired,
            turned,
            paired,
            turned,
            token,
        ),
        out_specs=(
            token,
            token,
            P(both, None, "tp"),
            P(None, both),
            weight,
            weight,
            paired,
            turned,
            weight,
            paired,
            turned,
            paired,
            turned,
        ),
        check_vma=False,
    )
```
